32 devices in a mesh: leaf: 4 (over x, core), chain: 8 (over z, y).
Axes of the slice: x: 2, y: 2, z: 4, core: 2. Of those that a mesh axis runs over, the one named last changes fastest.
Arguments:
- observations: float32 [32, 128], P(('chain', 'leaf')), may hold values from -6 to 6
- observed: int32 [32, 128], P(('chain', 'leaf')), may hold values 0 or 1
- gaps: float32 [32], P(('chain', 'leaf')), may hold values from 0.015625 to 0.09375
- site_cov: float32 [128, 128], replicated, may hold values from -1 to 1, as said below
Outputs:
- filtered_mean: float32 [32, 256], P(('chain', 'leaf'))
- filtered_cov: float32 [32, 256, 256], P(('chain', 'leaf'))
The draws below stay inside these ranges and needn't reach their ends.
Inputs may be any that keep to these rules, and one draw needn't show every extreme that they name: site_cov is symmetric with unit diagonal and positive definite.
All inputs are finite; a program needn't handle non-finite values. Where the reference program divides by a largest or mean magnitude, that divisor is 1e-20 or more. No bound on the sum of `observed` on one device may be relied on, other than what follows from the above.
Results may differ from the reference program's by a relative error of at most 0.0003.
Values sent between devices are 32-bit elements; how exact they have to be, the bound alone decides.
A program may use at most 128 MiB of HBM per device.

```python
import math
import jax
import jax.numpy as jnp
from jax import lax

SITES = 128
NEWTON = 13
STEPS = 32


def draw_site_cov(key, part):
    inner = jax.random.fold_in(key, 11)
    raw = jax.random.uniform(inner, (SITES, SITES), jnp.float32, -1.0, 1.0)
    off = 0.5 * (raw + raw.T) * (0.9 / SITES)
    eye = jnp.eye(SITES, dtype=jnp.float32)
    return eye + off * (1.0 - eye)


def place_ends(result, key, smallest, high):
    longest = result.shape.index(max(result.shape))
    spots = []
    for shift in (0, 1):
        where = [jax.random.randint(jax.random.fold_in(key, axis), (), 0, length) for axis, length in enumerate(result.shape)]
        where[longest] = (where[longest] + shift) % result.shape[longest]
        spots.append(tuple(where))
    return result.at[spots[0]].set(smallest).at[spots[1]].set(high)


def level_of(key, dims, pieces, low, largest):
    factor_of, own = 1.0, jax.random.fold_in(key, 6)
    for axis_at, parts in pieces:
        draws = jnp.exp(jax.random.uniform(jax.random.fold_in(own, axis_at), (parts,), jnp.float32, low / len(pieces), largest / len(pieces)))
        factor_of = factor_of * jnp.repeat(draws, dims[axis_at] // parts).reshape([-1 if axis == axis_at else 1 for axis in range(len(dims))])
    return factor_of


def bell_draw(rng, extent, deviation, bound, split=(), kind=jnp.bfloat16):
    values = deviation * jax.random.normal(rng, extent, jnp.float32)
    if split:
        values = values * level_of(rng, extent, split, -0.22, 0.18)
    return jnp.clip(values, -bound, bound).astype(kind)


def setup_inputs(seed: int = 0) -> dict:
    streams_of = jax.random.split(jax.random.key(seed), 5)
    observations = bell_draw(streams_of[0], (STEPS, SITES), 1.0, 6.0, ((0, 32),), jnp.float32)
    observed = place_ends((jax.random.randint(streams_of[1], (STEPS, SITES), 0, 8) < 1).astype(jnp.int32), jax.random.fold_in(streams_of[1], 1), 0, 1)
    gaps = jnp.clip(jnp.exp(math.log(0.09375) - 1.7917595 * jax.random.uniform(streams_of[2], (STEPS,), jnp.float32) ** level_of(streams_of[2], (STEPS,), ((0, 32),), -0.2, 0.2)), 0.015625, 0.09375)
    site_cov = draw_site_cov(jax.random.fold_in(streams_of[4], 71), 0)
    return {"observations": observations, "observed": observed, "gaps": gaps, "site_cov": site_cov}


HIGH = lax.Precision.HIGHEST
NOISE_VAR = 0.3
RATE = math.sqrt(3.0)
SERIES = (1.0, 1.0 / 4.0, 1.0 / 20.0, 1.0 / 120.0, 1.0 / 840.0, 1.0 / 6720.0, 1.0 / 60480.0, 1.0 / 604800.0)

def matmul(left, right):
    return jnp.matmul(left, right, precision=HIGH)

def flip(mat):
    return jnp.swapaxes(mat, -1, -2)

def inverse(mat):
    dim = mat.shape[-1]
    eye = jnp.eye(dim, dtype=mat.dtype)
    scale = 1.0 / lax.optimization_barrier(jnp.max(lax.optimization_barrier(jnp.sum(jnp.abs(mat), -1)), -1))
    approx = scale[..., None, None] * eye
    for turn in range(NEWTON):
        approx = matmul(approx, 2.0 * eye - matmul(mat, approx))
    return approx

def gamma_three(twice, square):
    total = jnp.zeros_like(twice) + SERIES[7]
    for coef in SERIES[6::-1]:
        total = total * twice + coef
    return square * twice * twice * twice / 6.0 * total

def form_elements(obs, mask, gap, cov, first):
    count = obs.shape[0]
    sites = cov.shape[0]
    dim = 2 * sites
    reach = RATE * gap
    decay = jnp.where(first, jnp.zeros_like(reach), jnp.exp(-reach))
    row_one = jnp.stack([decay * (1.0 + reach), decay * reach], -1)
    row_two = jnp.stack([-decay * reach, decay * (1.0 - reach)], -1)
    small = jnp.stack([row_one, row_two], -2)
    square = decay * decay
    corner = gamma_three(2.0 * reach, square)
    q_first = jnp.where(first, jnp.ones_like(reach), corner)
    q_cross = 2.0 * reach * reach * square
    q_last = 1.0 - square * (1.0 - 2.0 * reach + 2.0 * reach * reach)
    small_q = jnp.stack([jnp.stack([q_first, q_cross], -1), jnp.stack([q_cross, q_last], -1)], -2)
    eye_s = jnp.eye(sites, dtype=cov.dtype)
    trans = (eye_s[None, :, None, :, None] * small[:, None, :, None, :]).reshape(count, dim, dim)
    proc = (cov[None, :, None, :, None] * small_q[:, None, :, None, :]).reshape(count, dim, dim)
    weight = jnp.sqrt(mask.astype(cov.dtype) / NOISE_VAR)
    unit = jnp.stack([jnp.ones((), cov.dtype), jnp.zeros((), cov.dtype)])
    obs_map = (weight[:, :, None, None] * eye_s[None, :, :, None] * unit).reshape(count, sites, dim)
    hq = matmul(obs_map, proc)
    innov = eye_s + matmul(hq, flip(obs_map))
    inv_innov = inverse(innov)
    solved_h = matmul(inv_innov, obs_map)
    eye_d = jnp.eye(dim, dtype=cov.dtype)
    keep = eye_d - matmul(flip(hq), solved_h)
    trans_a = matmul(keep, trans)
    cov_c = matmul(keep, proc)
    cov_c = 0.5 * (cov_c + flip(cov_c))
    solved_y = matmul(inv_innov, (weight * obs)[..., None])
    mean_b = matmul(flip(hq), solved_y)[..., 0]
    hf = matmul(obs_map, trans)
    info_e = matmul(flip(hf), solved_y)[..., 0]
    info_j = matmul(flip(hf), matmul(solved_h, trans))
    valid = jnp.ones((count,), cov.dtype)
    return (trans_a, mean_b, cov_c, info_e, info_j, valid)

def expand(flag, value):
    return flag.reshape(flag.shape + (1,) * (value.ndim - flag.ndim))

def combine(early, late):
    aa, ba, ca, ea, ja, va = early
    ab, bb, cb, eb, jb, vb = late
    dim = aa.shape[-1]
    eye = jnp.eye(dim, dtype=aa.dtype)
    live_a = va > 0.5
    live_b = vb > 0.5
    system = eye + matmul(ca, jb)
    wmat = matmul(inverse(system), ca)
    wmat = 0.5 * (wmat + flip(wmat))
    keep = eye - matmul(wmat, jb)
    kept_a = matmul(keep, aa)
    new_a = matmul(ab, kept_a)
    inner = matmul(keep, ba[..., None]) + matmul(wmat, eb[..., None])
    new_b = matmul(ab, inner)[..., 0] + bb
    new_c = matmul(matmul(ab, wmat), flip(ab)) + cb
    gap_e = eb - matmul(jb, ba[..., None])[..., 0]
    new_e = matmul(flip(aa), matmul(flip(keep), gap_e[..., None]))[..., 0] + ea
    new_j = matmul(flip(aa), matmul(jb, kept_a)) + ja
    fresh = (new_a, new_b, new_c, new_e, new_j)
    picked = tuple((jnp.where(expand(live_b, x), jnp.where(expand(live_a, x), x, y), z) for x, y, z in zip(fresh, late[:5], early[:5])))
    return picked + (jnp.maximum(va, vb),)

def identity(dim, dtype):
    eye = jnp.eye(dim, dtype=dtype)
    zero_vec = jnp.zeros((dim,), dtype)
    zero_mat = jnp.zeros((dim, dim), dtype)
    return (eye, zero_vec, zero_mat, zero_vec, zero_mat, jnp.zeros((), dtype))

def reference(observations, observed, gaps, site_cov):
    steps = observations.shape[0]
    dim = 2 * site_cov.shape[0]
    first = jnp.arange(steps) == 0

    def advance(carry, inputs):
        obs, mask, gap, start = inputs
        elem = form_elements(obs[None], mask[None], gap[None], site_cov, start[None])
        elem = tuple((x[0] for x in elem))
        merged = combine(carry, elem)
        return (merged, (merged[1], merged[2]))
    _, outs = lax.scan(advance, identity(dim, site_cov.dtype), (observations, observed, gaps, first))
    return (outs[0], outs[1])
```

```python
import functools
import math

import jax
import jax.numpy as jnp
from jax import lax
from jax.experimental import pallas as pl
from jax.experimental.pallas import tpu as pltpu
from jax.sharding import PartitionSpec as P

NEWTON = 13
HIGH = lax.Precision.HIGHEST
NOISE_VAR = 0.3
RATE = math.sqrt(3.0)
SERIES = (
    1.0,
    1.0 / 4.0,
    1.0 / 20.0,
    1.0 / 120.0,
    1.0 / 840.0,
    1.0 / 6720.0,
    1.0 / 60480.0,
    1.0 / 604800.0,
)
SMALL = 4e-3
PAD = 8


def gamma_three(twice, square):
    total = jnp.zeros_like(twice) + SERIES[7]
    for coef in SERIES[6::-1]:
        total = total * twice + coef
    return square * twice * twice * twice / 6.0 * total


def exact(left, right):
    return jnp.dot(left, right, precision=HIGH, preferred_element_type=jnp.float32)


def fast(left, right):
    return jnp.dot(left, right, preferred_element_type=jnp.float32)


def split(x):
    high = x.astype(jnp.bfloat16)
    low = (x - high.astype(jnp.float32)).astype(jnp.bfloat16)
    return high, low


def filter_kernel(steps, count, place_ref, data_ref, cov_ref, mean_ref, out_ref,
                  coef, state, pred, left, power):
    sites = cov_ref.shape[0]
    dim = 2 * sites
    f32 = jnp.float32
    rows = lax.broadcasted_iota(jnp.int32, (sites, sites), 0)
    cols = lax.broadcasted_iota(jnp.int32, (sites, sites), 1)
    eye = (rows == cols).astype(f32)

    gap = data_ref[:, 2 * sites:]
    first = lax.broadcasted_iota(jnp.int32, gap.shape, 0) == 0
    reach = RATE * gap
    decay = jnp.where(first, 0.0, jnp.exp(-reach))
    square = decay * decay
    coef[0] = decay * (1.0 + reach)
    coef[1] = decay * reach
    coef[2] = -decay * reach
    coef[3] = decay * (1.0 - reach)
    coef[4] = jnp.where(first, 1.0, gamma_three(2.0 * reach, square))
    coef[5] = 2.0 * reach * reach * square
    coef[6] = 1.0 - square * (1.0 - 2.0 * reach + 2.0 * reach * reach)
    coef[7] = data_ref[:, sites:2 * sites] / NOISE_VAR
    coef[8] = data_ref[:, :sites]
    state[...] = jnp.zeros_like(state)
    start = place_ref[0] * count

    def step(k, _):
        row = pl.ds(k, 1)
        f00, f01, f10, f11 = (coef[i, row, :] for i in range(4))
        q00, q01, q11 = (coef[i, row, :] for i in range(4, 7))
        weight = coef[7, row, :]
        obs = coef[8, row, :]
        cov = cov_ref[...]

        spp, spv = state[:sites, :sites], state[:sites, sites:]
        svp, svv = state[sites:dim, :sites], state[sites:dim, sites:]
        smp, smv = state[dim:, :sites], state[dim:, sites:]
        lpp, lpv = f00 * spp + f01 * svp, f00 * spv + f01 * svv
        lvp, lvv = f10 * spp + f11 * svp, f10 * spv + f11 * svv
        ppp = f00 * lpp + f01 * lpv + q00 * cov
        ppv = f10 * lpp + f11 * lpv + q01 * cov
        pvp = f00 * lvp + f01 * lvv + q01 * cov
        pvv = f10 * lvp + f11 * lvv + q11 * cov
        pmp = f00 * smp + f01 * smv
        pmv = f10 * smp + f11 * smv
        pred[:sites, :sites] = ppp
        pred[:sites, sites:] = ppv
        pred[sites:dim, :sites] = pvp
        pred[sites:dim, sites:] = pvv
        pred[dim:, :sites] = pmp
        pred[dim:, sites:] = pmv

        diag = 1.0 + weight * jnp.sum(ppp * eye, axis=0, keepdims=True)
        scale = weight / diag
        r = (eye - 1.0) * ppp * scale
        y = jnp.concatenate([ppp * scale, pvp * scale, (pmp - obs) * scale], axis=0)
        rh, rl = split(r)
        yh, yl = split(y)
        r2 = fast(rh, rh)
        right = jnp.concatenate(
            [jnp.concatenate([rh, rl], axis=1)] * 2, axis=0)
        both = fast(jnp.concatenate([yh, yl], axis=1), right)
        y = y + (both[:, :sites] + both[:, sites:])
        trace = jnp.sum(r2 * eye)
        r2h = r2.astype(jnp.bfloat16)
        yh = y.astype(jnp.bfloat16)
        ph, pl_ = split(pred[:sites, :])
        u = fast(yh, r2h)
        z = fast(r2h, ph)
        y = y + u
        yh, yl = split(y)
        last = fast(
            jnp.concatenate([yh, yl, yh, u.astype(jnp.bfloat16)], axis=1),
            jnp.concatenate([ph, ph, pl_, z.astype(jnp.bfloat16)], axis=0))
        state[...] = pred[...] - last

        @pl.when(jnp.logical_not(trace < SMALL))
        def _():
            pp = pred[:sites, :sites]
            off = (1.0 - eye) * pp * scale
            reach_off = jnp.max(jnp.sum(jnp.abs(off), axis=0, keepdims=True), axis=1, keepdims=True)
            most = jnp.max(diag, axis=1, keepdims=True)
            low = jnp.maximum(1.0 / most, 1.0 - reach_off)
            omega = 2.0 / (low + 1.0 + reach_off)
            power[...] = (1.0 - omega) * eye - omega * off
            left[:dim, :] = omega * (pred[:dim, :sites] * scale)
            left[dim:, :] = omega * ((pred[dim:, :sites] - obs) * scale)

            def turn(i, _):
                now = power[...]
                left[...] = left[...] + exact(left[...], now)
                power[...] = exact(now, now)
                return 0

            lax.fori_loop(0, NEWTON, turn, 0)
            state[...] = pred[...] - exact(left[...], pred[:sites, :])

        @pl.when(k >= start)
        def _():
            source = lax.broadcasted_iota(jnp.int32, (dim, dim), 0)
            target = lax.broadcasted_iota(jnp.int32, (dim, dim), 1)
            move = (source == (target % 2) * sites + target // 2).astype(f32)
            wide = exact(state[...], move)
            source = lax.broadcasted_iota(jnp.int32, (dim, dim), 1)
            target = lax.broadcasted_iota(jnp.int32, (dim, dim), 0)
            back = (source == (target % 2) * sites + target // 2).astype(f32)
            out_ref[pl.ds(k - start, 1)] = exact(back, wide[:dim])[None]
            mean_ref[pl.ds(k - start, 1)] = wide[dim:dim + 1][None]

        return 0

    lax.fori_loop(0, start + count, step, 0)


def local(observations, observed, gaps, site_cov):
    count, sites = observations.shape
    dim = 2 * sites
    devices = lax.axis_size("leaf") * lax.axis_size("chain")
    place = lax.axis_index("chain") * lax.axis_size("leaf") + lax.axis_index("leaf")
    steps = count * devices
    packed = jnp.concatenate(
        [observations, observed.astype(jnp.float32),
         jnp.broadcast_to(gaps[:, None], (count, sites))], axis=1)
    data = lax.all_gather(packed, ("chain", "leaf"), axis=0, tiled=True)
    vmem = pl.BlockSpec(memory_space=pltpu.VMEM)
    mean, covs = pl.pallas_call(
        functools.partial(filter_kernel, steps, count),
        out_shape=(
            jax.ShapeDtypeStruct((count, 1, dim), jnp.float32),
            jax.ShapeDtypeStruct((count, dim, dim), jnp.float32),
        ),
        in_specs=[pl.BlockSpec(memory_space=pltpu.SMEM), vmem, vmem],
        out_specs=(vmem, vmem),
        scratch_shapes=[
            pltpu.VMEM((9, steps, sites), jnp.float32),
            pltpu.VMEM((dim + PAD, dim), jnp.float32),
            pltpu.VMEM((dim + PAD, dim), jnp.float32),
            pltpu.VMEM((dim + PAD, sites), jnp.float32),
            pltpu.VMEM((sites, sites), jnp.float32),
        ],
        compiler_params=pltpu.CompilerParams(vmem_limit_bytes=32 * 1024 * 1024),
    )(jnp.reshape(place, (1,)).astype(jnp.int32), data, site_cov)
    return mean.reshape(count, dim), covs


def solution(mesh):
    placed = (P(("chain", "leaf"), None), P(("chain", "leaf"), None), P(("chain", "leaf")), P())
    return jax.shard_map(
        local,
        mesh=mesh,
        in_specs=placed,
        out_specs=(P(("chain", "leaf"), None), P(("chain", "leaf"), None, None)),
        check_vma=False,
    )
```

```python
import functools
import math

import jax
import jax.numpy as jnp
from jax import lax
from jax.experimental import pallas as pl
from jax.experimental.pallas import tpu as pltpu
from jax.sharding import PartitionSpec as P

NEWTON = 13
HIGH = lax.Precision.HIGHEST
NOISE_VAR = 0.3
RATE = math.sqrt(3.0)
SERIES = (
    1.0,
    1.0 / 4.0,
    1.0 / 20.0,
    1.0 / 120.0,
    1.0 / 840.0,
    1.0 / 6720.0,
    1.0 / 60480.0,
    1.0 / 604800.0,
)
SMALL = 4e-3
PAD = 8


def gamma_three(twice, square):
    total = jnp.zeros_like(twice) + SERIES[7]
    for coef in SERIES[6::-1]:
        total = total * twice + coef
    return square * twice * twice * twice / 6.0 * total


def exact(left, right):
    return jnp.dot(left, right, precision=HIGH, preferred_element_type=jnp.float32)


def fast(left, right):
    return jnp.dot(left, right, preferred_element_type=jnp.float32)


def split(x):
    high = x.astype(jnp.bfloat16)
    low = (x - high.astype(jnp.float32)).astype(jnp.bfloat16)
    return high, low


def filter_kernel(steps, count, place_ref, data_ref, cov_ref, mean_ref, out_ref,
                  coef, state, pred, left, power):
    sites = cov_ref.shape[0]
    dim = 2 * sites
    f32 = jnp.float32
    rows = lax.broadcasted_iota(jnp.int32, (sites, sites), 0)
    cols = lax.broadcasted_iota(jnp.int32, (sites, sites), 1)
    eye = (rows == cols).astype(f32)

    for k in range(steps):
        for part, plane in ((0, 8), (1, 7), (2, 0)):
            coef[plane, pl.ds(k, 1), :] = data_ref[k // count, pl.ds(k % count, 1), pl.ds(part * sites, sites)]
    gap = coef[0]
    first = lax.broadcasted_iota(jnp.int32, gap.shape, 0) == 0
    reach = RATE * gap
    decay = jnp.where(first, 0.0, jnp.exp(-reach))
    square = decay * decay
    coef[0] = decay * (1.0 + reach)
    coef[1] = decay * reach
    coef[2] = -decay * reach
    coef[3] = decay * (1.0 - reach)
    coef[4] = jnp.where(first, 1.0, gamma_three(2.0 * reach, square))
    coef[5] = 2.0 * reach * reach * square
    coef[6] = 1.0 - square * (1.0 - 2.0 * reach + 2.0 * reach * reach)
    coef[7] = coef[7] / NOISE_VAR
    state[...] = jnp.zeros_like(state)
    start = place_ref[0] * count

    def step(k, _):
        row = pl.ds(k, 1)
        f00, f01, f10, f11 = (coef[i, row, :] for i in range(4))
        q00, q01, q11 = (coef[i, row, :] for i in range(4, 7))
        weight = coef[7, row, :]
        obs = coef[8, row, :]
        cov = cov_ref[...]

        spp, spv = state[:sites, :sites], state[:sites, sites:]
        svp, svv = state[sites:dim, :sites], state[sites:dim, sites:]
        smp, smv = state[dim:, :sites], state[dim:, sites:]
        lpp, lpv = f00 * spp + f01 * svp, f00 * spv + f01 * svv
        lvp, lvv = f10 * spp + f11 * svp, f10 * spv + f11 * svv
        ppp = f00 * lpp + f01 * lpv + q00 * cov
        ppv = f10 * lpp + f11 * lpv + q01 * cov
        pvp = f00 * lvp + f01 * lvv + q01 * cov
        pvv = f10 * lvp + f11 * lvv + q11 * cov
        pmp = f00 * smp + f01 * smv
        pmv = f10 * smp + f11 * smv
        pred[:sites, :sites] = ppp
        pred[:sites, sites:] = ppv
        pred[sites:dim, :sites] = pvp
        pred[sites:dim, sites:] = pvv
        pred[dim:, :sites] = pmp
        pred[dim:, sites:] = pmv

        diag = 1.0 + weight * jnp.sum(ppp * eye, axis=0, keepdims=True)
        scale = weight / diag
        r = (eye - 1.0) * ppp * scale
        y = jnp.concatenate([ppp * scale, pvp * scale, (pmp - obs) * scale], axis=0)
        rh, rl = split(r)
        yh, yl = split(y)
        r2 = fast(rh, rh)
        right = jnp.concatenate(
            [jnp.concatenate([rh, rl], axis=1)] * 2, axis=0)
        both = fast(jnp.concatenate([yh, yl], axis=1), right)
        y = y + (both[:, :sites] + both[:, sites:])
        trace = jnp.sum(r2 * eye)
        r2h = r2.astype(jnp.bfloat16)
        yh = y.astype(jnp.bfloat16)
        ph, pl_ = split(pred[:sites, :])
        u = fast(yh, r2h)
        z = fast(r2h, ph)
        y = y + u
        yh, yl = split(y)
        last = fast(
            jnp.concatenate([yh, yl, yh, u.astype(jnp.bfloat16)], axis=1),
            jnp.concatenate([ph, ph, pl_, z.astype(jnp.bfloat16)], axis=0))
        state[...] = pred[...] - last

        @pl.when(jnp.logical_not(trace < SMALL))
        def _():
            pp = pred[:sites, :sites]
            off = (1.0 - eye) * pp * scale
            reach_off = jnp.max(jnp.sum(jnp.abs(off), axis=0, keepdims=True), axis=1, keepdims=True)
            most = jnp.max(diag, axis=1, keepdims=True)
            low = jnp.maximum(1.0 / most, 1.0 - reach_off)
            omega = 2.0 / (low + 1.0 + reach_off)
            power[...] = (1.0 - omega) * eye - omega * off
            left[:dim, :] = omega * (pred[:dim, :sites] * scale)
            left[dim:, :] = omega * ((pred[dim:, :sites] - obs) * scale)

            def turn(i, _):
                now = power[...]
                left[...] = left[...] + exact(left[...], now)
                power[...] = exact(now, now)
                return 0

            lax.fori_loop(0, NEWTON, turn, 0)
            state[...] = pred[...] - exact(left[...], pred[:sites, :])

        @pl.when(k >= start)
        def _():
            source = lax.broadcasted_iota(jnp.int32, (dim, dim), 0)
            target = lax.broadcasted_iota(jnp.int32, (dim, dim), 1)
            move = (source == (target % 2) * sites + target // 2).astype(f32)
            wide = exact(state[...], move)
            source = lax.broadcasted_iota(jnp.int32, (dim, dim), 1)
            target = lax.broadcasted_iota(jnp.int32, (dim, dim), 0)
            back = (source == (target % 2) * sites + target // 2).astype(f32)
            out_ref[pl.ds(k - start, 1)] = exact(back, wide[:dim])[None]
            mean_ref[pl.ds(k - start, 1)] = wide[dim:dim + 1][None]

        return 0

    lax.fori_loop(0, start + count, step, 0)


def gather_kernel(chains, leaves, mine_ref, all_ref, own_sem, leaf_send, leaf_recv, chain_send, chain_recv):
    leaf = lax.axis_index("leaf")
    chain = lax.axis_index("chain")
    barrier = pltpu.get_barrier_semaphore()
    for turn in range(1, chains):
        there = lax.rem(chain + turn, chains)
        pl.semaphore_signal(barrier, inc=1, device_id={"chain": there}, device_id_type=pl.DeviceIdType.MESH)
    for turn in range(1, leaves):
        there = lax.rem(leaf + turn, leaves)
        pl.semaphore_signal(barrier, inc=1, device_id={"leaf": there}, device_id_type=pl.DeviceIdType.MESH)
    own = pltpu.make_async_copy(mine_ref, all_ref.at[chain, leaf], own_sem)
    own.start()
    pl.semaphore_wait(barrier, chains + leaves - 2)

    sends = []
    for turn in range(1, leaves):
        copy = pltpu.make_async_remote_copy(
            src_ref=mine_ref,
            dst_ref=all_ref.at[chain, leaf],
            send_sem=leaf_send.at[turn - 1],
            recv_sem=leaf_recv.at[turn - 1],
            device_id={"leaf": lax.rem(leaf + turn, leaves)},
            device_id_type=pl.DeviceIdType.MESH,
        )
        copy.start()
        sends.append(copy)
    own.wait()
    for copy in sends:
        copy.wait_recv()
    later = []
    for turn in range(chains - 1, 0, -1):
        copy = pltpu.make_async_remote_copy(
            src_ref=all_ref.at[chain],
            dst_ref=all_ref.at[chain],
            send_sem=chain_send.at[turn - 1],
            recv_sem=chain_recv.at[turn - 1],
            device_id={"chain": lax.rem(chain + turn, chains)},
            device_id_type=pl.DeviceIdType.MESH,
        )
        copy.start()
        later.append(copy)
    for copy in later:
        copy.wait_recv()
    for copy in sends + later:
        copy.wait_send()


def gathered(packed):
    leaves = lax.axis_size("leaf")
    chains = lax.axis_size("chain")
    vmem = pl.BlockSpec(memory_space=pltpu.VMEM)
    dma = pltpu.SemaphoreType.DMA
    return pl.pallas_call(
        functools.partial(gather_kernel, chains, leaves),
        out_shape=jax.ShapeDtypeStruct((chains, leaves) + packed.shape, packed.dtype),
        in_specs=[vmem],
        out_specs=vmem,
        scratch_shapes=[dma, dma((leaves - 1,)), dma((leaves - 1,)), dma((chains - 1,)), dma((chains - 1,))],
        compiler_params=pltpu.CompilerParams(collective_id=0, has_side_effects=True),
    )(packed)


def local(observations, observed, gaps, site_cov):
    count, sites = observations.shape
    dim = 2 * sites
    devices = lax.axis_size("leaf") * lax.axis_size("chain")
    place = lax.axis_index("chain") * lax.axis_size("leaf") + lax.axis_index("leaf")
    steps = count * devices
    packed = jnp.concatenate(
        [observations, observed.astype(jnp.float32),
         jnp.broadcast_to(gaps[:, None], (count, sites))], axis=1)
    data = gathered(packed).reshape(devices, count, 3 * sites)
    vmem = pl.BlockSpec(memory_space=pltpu.VMEM)
    mean, covs = pl.pallas_call(
        functools.partial(filter_kernel, steps, count),
        out_shape=(
            jax.ShapeDtypeStruct((count, 1, dim), jnp.float32),
            jax.ShapeDtypeStruct((count, dim, dim), jnp.float32),
        ),
        in_specs=[pl.BlockSpec(memory_space=pltpu.SMEM), vmem, vmem],
        out_specs=(vmem, vmem),
        scratch_shapes=[
            pltpu.VMEM((9, steps, sites), jnp.float32),
            pltpu.VMEM((dim + PAD, dim), jnp.float32),
            pltpu.VMEM((dim + PAD, dim), jnp.float32),
            pltpu.VMEM((dim + PAD, sites), jnp.float32),
            pltpu.VMEM((sites, sites), jnp.float32),
        ],
        compiler_params=pltpu.CompilerParams(vmem_limit_bytes=32 * 1024 * 1024),
    )(jnp.reshape(place, (1,)).astype(jnp.int32), data, site_cov)
    return mean.reshape(count, dim), covs


def solution(mesh):
    placed = (P(("chain", "leaf"), None), P(("chain", "leaf"), None), P(("chain", "leaf")), P())
    return jax.shard_map(
        local,
        mesh=mesh,
        in_specs=placed,
        out_specs=(P(("chain", "leaf"), None), P(("chain", "leaf"), None, None)),
        check_vma=False,
    )
```

```python
import functools
import math

import jax
import jax.numpy as jnp
from jax import lax
from jax.experimental import pallas as pl
from jax.experimental.pallas import tpu as pltpu
from jax.sharding import PartitionSpec as P

NEWTON = 13
HIGH = lax.Precision.HIGHEST
NOISE_VAR = 0.3
RATE = math.sqrt(3.0)
SERIES = (
    1.0,
    1.0 / 4.0,
    1.0 / 20.0,
    1.0 / 120.0,
    1.0 / 840.0,
    1.0 / 6720.0,
    1.0 / 60480.0,
    1.0 / 604800.0,
)
SMALL = 4e-3
PAD = 8


def gamma_three(twice, square):
    total = jnp.zeros_like(twice) + SERIES[7]
    for coef in SERIES[6::-1]:
        total = total * twice + coef
    return square * twice * twice * twice / 6.0 * total


def exact(left, right):
    return jnp.dot(left, right, precision=HIGH, preferred_element_type=jnp.float32)


def fast(left, right):
    return jnp.dot(left, right, preferred_element_type=jnp.float32)


def split(x):
    high = x.astype(jnp.bfloat16)
    low = (x - high.astype(jnp.float32)).astype(jnp.bfloat16)
    return high, low


def filter_kernel(steps, count, place_ref, data_ref, cov_ref, mean_ref, out_ref,
                  coef, state, pred, left, power, woven):
    sites = cov_ref.shape[0]
    dim = 2 * sites
    f32 = jnp.float32
    rows = lax.broadcasted_iota(jnp.int32, (sites, sites), 0)
    cols = lax.broadcasted_iota(jnp.int32, (sites, sites), 1)
    eye = (rows == cols).astype(f32)
    apart = (rows != cols).astype(f32).astype(jnp.bfloat16)

    for k in range(steps):
        for part, plane in ((0, 8), (1, 7), (2, 0)):
            coef[plane, pl.ds(k, 1), :] = data_ref[k // count, pl.ds(k % count, 1), pl.ds(part * sites, sites)]
    gap = coef[0]
    first = lax.broadcasted_iota(jnp.int32, gap.shape, 0) == 0
    reach = RATE * gap
    decay = jnp.where(first, 0.0, jnp.exp(-reach))
    square = decay * decay
    coef[0] = decay * (1.0 + reach)
    coef[1] = decay * reach
    coef[2] = -decay * reach
    coef[3] = decay * (1.0 - reach)
    coef[4] = jnp.where(first, 1.0, gamma_three(2.0 * reach, square))
    coef[5] = 2.0 * reach * reach * square
    coef[6] = 1.0 - square * (1.0 - 2.0 * reach + 2.0 * reach * reach)
    coef[7] = coef[7] / NOISE_VAR
    state[...] = jnp.zeros_like(state)
    start = place_ref[0] * count

    def step(k, _):
        row = pl.ds(k, 1)
        f00, f01, f10, f11 = (coef[i, row, :] for i in range(4))
        q00, q01, q11 = (coef[i, row, :] for i in range(4, 7))
        weight = coef[7, row, :]
        obs = coef[8, row, :]
        cov = cov_ref[...]

        spp, spv = state[:sites, :sites], state[:sites, sites:]
        svp, svv = state[sites:dim, :sites], state[sites:dim, sites:]
        smp, smv = state[dim:, :sites], state[dim:, sites:]
        lpp, lpv = f00 * spp + f01 * svp, f00 * spv + f01 * svv
        lvp, lvv = f10 * spp + f11 * svp, f10 * spv + f11 * svv
        ppp = f00 * lpp + f01 * lpv + q00 * cov
        ppv = f10 * lpp + f11 * lpv + q01 * cov
        pvp = f00 * lvp + f01 * lvv + q01 * cov
        pvv = f10 * lvp + f11 * lvv + q11 * cov
        pmp = f00 * smp + f01 * smv
        pmv = f10 * smp + f11 * smv
        pred[:sites, :sites] = ppp
        pred[:sites, sites:] = ppv
        pred[sites:dim, :sites] = pvp
        pred[sites:dim, sites:] = pvv
        pred[dim:, :sites] = pmp
        pred[dim:, sites:] = pmv

        diag = 1.0 + weight * jnp.sum(ppp * eye, axis=0, keepdims=True)
        scale = weight / diag
        y = jnp.concatenate([ppp * scale, pvp * scale, (pmp - obs) * scale], axis=0)
        yh, yl = split(y)
        rh, rl = yh[:sites] * apart, yl[:sites] * apart
        r2 = fast(rh, rh)
        right = jnp.concatenate(
            [jnp.concatenate([rh, rl], axis=1)] * 2, axis=0)
        both = fast(jnp.concatenate([yh, yl], axis=1), right)
        y = y - (both[:, :sites] + both[:, sites:])
        trace = jnp.sum(r2 * eye)
        r2h = r2.astype(jnp.bfloat16)
        ph, pl_ = split(pred[:sites, :])
        yh, yl = split(y)
        z = fast(r2h, ph)
        u = fast(yh, r2h)
        main = fast(
            jnp.concatenate([yh, yl, yh], axis=1),
            jnp.concatenate([ph, ph, pl_], axis=0))
        rest = fast(u.astype(jnp.bfloat16), (pred[:sites, :] + z).astype(jnp.bfloat16))
        state[...] = (pred[...] - main) - rest

        @pl.when(jnp.logical_not(trace < SMALL))
        def _():
            pp = pred[:sites, :sites]
            off = (1.0 - eye) * pp * scale
            reach_off = jnp.max(jnp.sum(jnp.abs(off), axis=0, keepdims=True), axis=1, keepdims=True)
            most = jnp.max(diag, axis=1, keepdims=True)
            low = jnp.maximum(1.0 / most, 1.0 - reach_off)
            omega = 2.0 / (low + 1.0 + reach_off)
            power[...] = (1.0 - omega) * eye - omega * off
            left[:dim, :] = omega * (pred[:dim, :sites] * scale)
            left[dim:, :] = omega * ((pred[dim:, :sites] - obs) * scale)

            def turn(i, _):
                now = power[...]
                left[...] = left[...] + exact(left[...], now)
                power[...] = exact(now, now)
                return 0

            lax.fori_loop(0, NEWTON, turn, 0)
            state[...] = pred[...] - exact(left[...], pred[:sites, :])

        @pl.when(k >= start)
        def _():
            source = lax.broadcasted_iota(jnp.int32, (dim, dim), 0)
            target = lax.broadcasted_iota(jnp.int32, (dim, dim), 1)
            move = (source == (target % 2) * sites + target // 2).astype(f32)
            high, low = split(state[...])
            tail = ((state[...] - high.astype(f32)) - low.astype(f32)).astype(jnp.bfloat16)
            move = move.astype(jnp.bfloat16)
            wide = fast(
                jnp.concatenate([high, low, tail], axis=1),
                jnp.concatenate([move, move, move], axis=0))
            for part in range(2):
                half = pl.ds(part * sites, sites)
                woven[pl.ds(0, sites, stride=2), :] = wide[:sites, part * sites:(part + 1) * sites]
                woven[pl.ds(1, sites, stride=2), :] = wide[sites:dim, part * sites:(part + 1) * sites]
                out_ref[pl.ds(k - start, 1), :, half] = woven[...][None]
            mean_ref[pl.ds(k - start, 1)] = wide[dim:dim + 1][None]

        return 0

    lax.fori_loop(0, start + count, step, 0)


def gather_kernel(chains, leaves, obs_ref, seen_ref, gap_ref, all_ref, mine_ref, own_sem, leaf_send, leaf_recv, chain_send, chain_recv):
    leaf = lax.axis_index("leaf")
    chain = lax.axis_index("chain")
    barrier = pltpu.get_barrier_semaphore()
    for turn in range(1, chains):
        there = lax.rem(chain + turn, chains)
        pl.semaphore_signal(barrier, inc=1, device_id={"chain": there}, device_id_type=pl.DeviceIdType.MESH)
    for turn in range(1, leaves):
        there = lax.rem(leaf + turn, leaves)
        pl.semaphore_signal(barrier, inc=1, device_id={"leaf": there}, device_id_type=pl.DeviceIdType.MESH)
    count, sites = obs_ref.shape
    mine_ref[:, :sites] = obs_ref[...]
    mine_ref[:, sites:2 * sites] = seen_ref[...].astype(jnp.float32)
    for i in range(count):
        mine_ref[i:i + 1, 2 * sites:] = jnp.full((1, sites), gap_ref[i], jnp.float32)
    own = pltpu.make_async_copy(mine_ref, all_ref.at[chain, leaf], own_sem)
    own.start()
    pl.semaphore_wait(barrier, chains + leaves - 2)

    sends = []
    for turn in range(1, leaves):
        copy = pltpu.make_async_remote_copy(
            src_ref=mine_ref,
            dst_ref=all_ref.at[chain, leaf],
            send_sem=leaf_send.at[turn - 1],
            recv_sem=leaf_recv.at[turn - 1],
            device_id={"leaf": lax.rem(leaf + turn, leaves)},
            device_id_type=pl.DeviceIdType.MESH,
        )
        copy.start()
        sends.append(copy)
    own.wait()
    for copy in sends:
        copy.wait_recv()
    later = []
    for turn in range(chains - 1, 0, -1):
        copy = pltpu.make_async_remote_copy(
            src_ref=all_ref.at[chain],
            dst_ref=all_ref.at[chain],
            send_sem=chain_send.at[turn - 1],
            recv_sem=chain_recv.at[turn - 1],
            device_id={"chain": lax.rem(chain + turn, chains)},
            device_id_type=pl.DeviceIdType.MESH,
        )
        copy.start()
        later.append(copy)
    for copy in later:
        copy.wait_recv()
    for copy in sends + later:
        copy.wait_send()


def gathered(observations, observed, gaps):
    leaves = lax.axis_size("leaf")
    chains = lax.axis_size("chain")
    count, sites = observations.shape
    vmem = pl.BlockSpec(memory_space=pltpu.VMEM)
    dma = pltpu.SemaphoreType.DMA
    return pl.pallas_call(
        functools.partial(gather_kernel, chains, leaves),
        out_shape=jax.ShapeDtypeStruct((chains, leaves, count, 3 * sites), jnp.float32),
        in_specs=[vmem, vmem, pl.BlockSpec(memory_space=pltpu.SMEM)],
        out_specs=vmem,
        scratch_shapes=[
            pltpu.VMEM((count, 3 * sites), jnp.float32),
            dma, dma((leaves - 1,)), dma((leaves - 1,)), dma((chains - 1,)), dma((chains - 1,)),
        ],
        compiler_params=pltpu.CompilerParams(collective_id=0, has_side_effects=True),
    )(observations, observed, gaps)


def run_filter(place, data, site_cov, steps, count):
    sites = site_cov.shape[0]
    dim = 2 * sites
    vmem = pl.BlockSpec(memory_space=pltpu.VMEM)
    return pl.pallas_call(
        functools.partial(filter_kernel, steps, count),
        out_shape=(
            jax.ShapeDtypeStruct((count, 1, dim), jnp.float32),
            jax.ShapeDtypeStruct((count, dim, dim), jnp.float32),
        ),
        in_specs=[pl.BlockSpec(memory_space=pltpu.SMEM), vmem, vmem],
        out_specs=(vmem, vmem),
        scratch_shapes=[
            pltpu.VMEM((9, steps, sites), jnp.float32),
            pltpu.VMEM((dim + PAD, dim), jnp.float32),
            pltpu.VMEM((dim + PAD, dim), jnp.float32),
            pltpu.VMEM((dim + PAD, sites), jnp.float32),
            pltpu.VMEM((sites, sites), jnp.float32),
            pltpu.VMEM((dim, sites), jnp.float32),
        ],
        compiler_params=pltpu.CompilerParams(vmem_limit_bytes=32 * 1024 * 1024),
    )(place, data, site_cov)


def local(observations, observed, gaps, site_cov):
    count, sites = observations.shape
    dim = 2 * sites
    devices = lax.axis_size("leaf") * lax.axis_size("chain")
    place = lax.axis_index("chain") * lax.axis_size("leaf") + lax.axis_index("leaf")
    steps = count * devices
    data = gathered(observations, observed, gaps).reshape(devices, count, 3 * sites)
    mean, covs = run_filter(jnp.reshape(place, (1,)).astype(jnp.int32), data, site_cov, steps, count)
    return mean.reshape(count, dim), covs


def solution(mesh):
    placed = (P(("chain", "leaf"), None), P(("chain", "leaf"), None), P(("chain", "leaf")), P())
    return jax.shard_map(
        local,
        mesh=mesh,
        in_specs=placed,
        out_specs=(P(("chain", "leaf"), None), P(("chain", "leaf"), None, None)),
        check_vma=False,
    )
```

```python
import functools
import math

import jax
import jax.numpy as jnp
from jax import lax
from jax.experimental import pallas as pl
from jax.experimental.pallas import tpu as pltpu
from jax.sharding import PartitionSpec as P

NEWTON = 13
HIGH = lax.Precision.HIGHEST
NOISE_VAR = 0.3
RATE = math.sqrt(3.0)
SERIES = (
    1.0,
    1.0 / 4.0,
    1.0 / 20.0,
    1.0 / 120.0,
    1.0 / 840.0,
    1.0 / 6720.0,
    1.0 / 60480.0,
    1.0 / 604800.0,
)
SMALL = 4e-3
PAD = 8


def gamma_three(twice, square):
    total = jnp.zeros_like(twice) + SERIES[7]
    for coef in SERIES[6::-1]:
        total = total * twice + coef
    return square * twice * twice * twice / 6.0 * total


def exact(left, right):
    return jnp.dot(left, right, precision=HIGH, preferred_element_type=jnp.float32)


def fast(left, right):
    return jnp.dot(left, right, preferred_element_type=jnp.float32)


def split(x):
    high = x.astype(jnp.bfloat16)
    low = (x - high.astype(jnp.float32)).astype(jnp.bfloat16)
    return high, low


def filter_kernel(steps, count, place_ref, data_ref, cov_ref, mean_ref, out_ref,
                  coef, state, pred, left, power, woven):
    sites = cov_ref.shape[0]
    dim = 2 * sites
    f32 = jnp.float32
    rows = lax.broadcasted_iota(jnp.int32, (sites, sites), 0)
    cols = lax.broadcasted_iota(jnp.int32, (sites, sites), 1)
    eye = (rows == cols).astype(f32)
    apart = (rows != cols).astype(f32).astype(jnp.bfloat16)

    for k in range(steps):
        for part, plane in ((0, 8), (1, 7), (2, 0)):
            coef[plane, pl.ds(k, 1), :] = data_ref[k // count, pl.ds(k % count, 1), pl.ds(part * sites, sites)]
    gap = coef[0]
    first = lax.broadcasted_iota(jnp.int32, gap.shape, 0) == 0
    reach = RATE * gap
    decay = jnp.where(first, 0.0, jnp.exp(-reach))
    square = decay * decay
    coef[0] = decay * (1.0 + reach)
    coef[1] = decay * reach
    coef[2] = -decay * reach
    coef[3] = decay * (1.0 - reach)
    coef[4] = jnp.where(first, 1.0, gamma_three(2.0 * reach, square))
    coef[5] = 2.0 * reach * reach * square
    coef[6] = 1.0 - square * (1.0 - 2.0 * reach + 2.0 * reach * reach)
    coef[7] = coef[7] / NOISE_VAR
    state[...] = jnp.zeros_like(state)
    start = place_ref[0] * count

    def step(k, _):
        row = pl.ds(k, 1)
        f00, f01, f10, f11 = (coef[i, row, :] for i in range(4))
        q00, q01, q11 = (coef[i, row, :] for i in range(4, 7))
        weight = coef[7, row, :]
        obs = coef[8, row, :]
        cov = cov_ref[...]

        spp, spv = state[:sites, :sites], state[:sites, sites:]
        svp, svv = state[sites:dim, :sites], state[sites:dim, sites:]
        smp, smv = state[dim:, :sites], state[dim:, sites:]
        lpp, lpv = f00 * spp + f01 * svp, f00 * spv + f01 * svv
        lvp, lvv = f10 * spp + f11 * svp, f10 * spv + f11 * svv
        ppp = f00 * lpp + f01 * lpv + q00 * cov
        ppv = f10 * lpp + f11 * lpv + q01 * cov
        pvp = f00 * lvp + f01 * lvv + q01 * cov
        pvv = f10 * lvp + f11 * lvv + q11 * cov
        pmp = f00 * smp + f01 * smv
        pmv = f10 * smp + f11 * smv
        pred[:sites, :sites] = ppp
        pred[:sites, sites:] = ppv
        pred[sites:dim, :sites] = pvp
        pred[sites:dim, sites:] = pvv
        pred[dim:, :sites] = pmp
        pred[dim:, sites:] = pmv

        diag = 1.0 + weight * jnp.sum(ppp * eye, axis=0, keepdims=True)
        scale = weight / diag
        y = jnp.concatenate([ppp * scale, pvp * scale, (pmp - obs) * scale], axis=0)
        yh, yl = split(y)
        rh, rl = yh[:sites] * apart, yl[:sites] * apart
        r2 = fast(rh, rh)
        right = jnp.concatenate(
            [jnp.concatenate([rh, rl], axis=1)] * 2, axis=0)
        both = fast(jnp.concatenate([yh, yl], axis=1), right)
        y = y - (both[:, :sites] + both[:, sites:])
        trace = jnp.sum(r2 * eye)
        r2h = r2.astype(jnp.bfloat16)
        ph, pl_ = split(pred[:sites, :])
        yh, yl = split(y)
        z = fast(r2h, ph)
        u = fast(yh, r2h)
        main = fast(
            jnp.concatenate([yh, yl, yh], axis=1),
            jnp.concatenate([ph, ph, pl_], axis=0))
        rest = fast(u.astype(jnp.bfloat16), (pred[:sites, :] + z).astype(jnp.bfloat16))
        state[...] = (pred[...] - main) - rest

        @pl.when(jnp.logical_not(trace < SMALL))
        def _():
            pp = pred[:sites, :sites]
            off = (1.0 - eye) * pp * scale
            reach_off = jnp.max(jnp.sum(jnp.abs(off), axis=0, keepdims=True), axis=1, keepdims=True)
            most = jnp.max(diag, axis=1, keepdims=True)
            low = jnp.maximum(1.0 / most, 1.0 - reach_off)
            omega = 2.0 / (low + 1.0 + reach_off)
            power[...] = (1.0 - omega) * eye - omega * off
            left[:dim, :] = omega * (pred[:dim, :sites] * scale)
            left[dim:, :] = omega * ((pred[dim:, :sites] - obs) * scale)

            def turn(i, _):
                now = power[...]
                left[...] = left[...] + exact(left[...], now)
                power[...] = exact(now, now)
                return 0

            lax.fori_loop(0, NEWTON, turn, 0)
            state[...] = pred[...] - exact(left[...], pred[:sites, :])

        @pl.when(k >= start)
        def _():
            source = lax.broadcasted_iota(jnp.int32, (dim, dim), 0)
            target = lax.broadcasted_iota(jnp.int32, (dim, dim), 1)
            move = (source == (target % 2) * sites + target // 2).astype(f32)
            high, low = split(state[...])
            tail = ((state[...] - high.astype(f32)) - low.astype(f32)).astype(jnp.bfloat16)
            move = move.astype(jnp.bfloat16)
            wide = fast(
                jnp.concatenate([high, low, tail], axis=1),
                jnp.concatenate([move, move, move], axis=0))
            for part in range(2):
                half = pl.ds(part * sites, sites)
                woven[pl.ds(0, sites, stride=2), :] = wide[:sites, part * sites:(part + 1) * sites]
                woven[pl.ds(1, sites, stride=2), :] = wide[sites:dim, part * sites:(part + 1) * sites]
                out_ref[pl.ds(k - start, 1), :, half] = woven[...][None]
            mean_ref[pl.ds(k - start, 1)] = wide[dim:dim + 1][None]

        return 0

    lax.fori_loop(0, start + count, step, 0)


def gather_kernel(chains, leaves, obs_ref, seen_ref, gap_ref, all_ref, mine_ref, own_sem, send_sem, recv_sem):
    total = chains * leaves
    chain = lax.axis_index("chain")
    leaf = lax.axis_index("leaf")
    me = chain * leaves + leaf
    barrier = pltpu.get_barrier_semaphore()

    def device(there):
        return {"chain": there // leaves, "leaf": lax.rem(there, leaves)}

    for turn in range(total - 1, 0, -1):
        @pl.when(me >= turn)
        def _():
            pl.semaphore_signal(barrier, inc=1, device_id=device(me - turn), device_id_type=pl.DeviceIdType.MESH)

    count, sites = obs_ref.shape
    mine_ref[:, :sites] = obs_ref[...]
    mine_ref[:, sites:2 * sites] = seen_ref[...].astype(jnp.float32)
    for i in range(count):
        mine_ref[i:i + 1, 2 * sites:] = jnp.full((1, sites), gap_ref[i], jnp.float32)
    own = pltpu.make_async_copy(mine_ref, all_ref.at[chain, leaf], own_sem)
    own.start()
    @pl.when(me < total - 1)
    def _():
        pl.semaphore_wait(barrier, total - 1 - me)

    def sent(turn):
        return pltpu.make_async_remote_copy(
            src_ref=mine_ref,
            dst_ref=all_ref.at[chain, leaf],
            send_sem=send_sem.at[turn - 1],
            recv_sem=recv_sem.at[turn - 1],
            device_id=device(lax.rem(me + turn, total)),
            device_id_type=pl.DeviceIdType.MESH,
        )

    for turn in range(total - 1, 0, -1):
        @pl.when(me + turn < total)
        def _():
            sent(turn).start()
    own.wait()
    for turn in range(total - 1, 0, -1):
        @pl.when(me >= turn)
        def _():
            sent(turn).wait_recv()

        @pl.when(me + turn < total)
        def _():
            sent(turn).wait_send()


def gathered(observations, observed, gaps):
    leaves = lax.axis_size("leaf")
    chains = lax.axis_size("chain")
    count, sites = observations.shape
    vmem = pl.BlockSpec(memory_space=pltpu.VMEM)
    dma = pltpu.SemaphoreType.DMA
    return pl.pallas_call(
        functools.partial(gather_kernel, chains, leaves),
        out_shape=jax.ShapeDtypeStruct((chains, leaves, count, 3 * sites), jnp.float32),
        in_specs=[vmem, vmem, pl.BlockSpec(memory_space=pltpu.SMEM)],
        out_specs=vmem,
        scratch_shapes=[
            pltpu.VMEM((count, 3 * sites), jnp.float32),
            dma, dma((chains * leaves - 1,)), dma((chains * leaves - 1,)),
        ],
        compiler_params=pltpu.CompilerParams(collective_id=0, has_side_effects=True),
    )(observations, observed, gaps)


def run_filter(place, data, site_cov, steps, count):
    sites = site_cov.shape[0]
    dim = 2 * sites
    vmem = pl.BlockSpec(memory_space=pltpu.VMEM)
    return pl.pallas_call(
        functools.partial(filter_kernel, steps, count),
        out_shape=(
            jax.ShapeDtypeStruct((count, 1, dim), jnp.float32),
            jax.ShapeDtypeStruct((count, dim, dim), jnp.float32),
        ),
        in_specs=[pl.BlockSpec(memory_space=pltpu.SMEM), vmem, vmem],
        out_specs=(vmem, vmem),
        scratch_shapes=[
            pltpu.VMEM((9, steps, sites), jnp.float32),
            pltpu.VMEM((dim + PAD, dim), jnp.float32),
            pltpu.VMEM((dim + PAD, dim), jnp.float32),
            pltpu.VMEM((dim + PAD, sites), jnp.float32),
            pltpu.VMEM((sites, sites), jnp.float32),
            pltpu.VMEM((dim, sites), jnp.float32),
        ],
        compiler_params=pltpu.CompilerParams(vmem_limit_bytes=32 * 1024 * 1024),
    )(place, data, site_cov)


def local(observations, observed, gaps, site_cov):
    count, sites = observations.shape
    dim = 2 * sites
    devices = lax.axis_size("leaf") * lax.axis_size("chain")
    place = lax.axis_index("chain") * lax.axis_size("leaf") + lax.axis_index("leaf")
    steps = count * devices
    data = gathered(observations, observed, gaps).reshape(devices, count, 3 * sites)
    mean, covs = run_filter(jnp.reshape(place, (1,)).astype(jnp.int32), data, site_cov, steps, count)
    return mean.reshape(count, dim), covs


def solution(mesh):
    placed = (P(("chain", "leaf"), None), P(("chain", "leaf"), None), P(("chain", "leaf")), P())
    return jax.shard_map(
        local,
        mesh=mesh,
        in_specs=placed,
        out_specs=(P(("chain", "leaf"), None), P(("chain", "leaf"), None, None)),
        check_vma=False,
    )
```
